512 devices in a mesh: batch: 32 (over x, z_lo), tensor: 16 (over y, z_hi, core).
Axes of the slice: x: 4, y: 4, z: 16 (z_hi: 2, z_lo: 8; z = z_hi * 8 + z_lo), core: 2. Of those that a mesh axis runs over, the one named last changes fastest.
Arguments:
- hidden_in: bfloat16 [16384, 8192], P('batch', 'tensor'), may hold values from -1600 to 1600, as said below
- norm_gain: bfloat16 [8192], P('tensor'), may hold values from 0.099609375 to 1.8984375
- q_weight: bfloat16 [8192, 4096], P(('batch', 'tensor')), may hold values from -0.4087961 to 0.4087961, as said below
- k_weight: bfloat16 [8192, 512], P(('batch', 'tensor')), may hold values from -0.044194174 to 0.044194174, as said below
- v_weight: bfloat16 [8192, 512], P(('batch', 'tensor')), may hold values from -0.0625 to 0.0625
Outputs:
- head_out: bfloat16 [16384, 4096], P('batch', 'tensor')
The draws below stay inside these ranges and needn't reach their ends.
Inputs may be any that keep to these rules, and one draw needn't show every extreme that they name: `hidden_in`: activations with independent scales over rows and over features. `q_weight`: A dense matrix. `k_weight`: A dense matrix.
All inputs are finite; a program needn't handle non-finite values.
Results may differ from the reference program's by a relative error of at most 0.008.
Values may be sent and summed in bfloat16 or wider, within the bound.
A program may use at most 128 MiB of HBM per device.

```python
import math
import jax
import jax.numpy as jnp
from jax import lax

D = 8192
HD = 128
QH = 32
KVH = 4
SEQ = 512
TOKENS = 16384


def draw_hidden_in(key, part):
    key_base = jax.random.fold_in(key, 11)
    key_rows = jax.random.fold_in(key, 12)
    key_cols = jax.random.fold_in(key, 13)
    row_scale = jnp.exp(jax.random.uniform(key_rows, (TOKENS, 1), jnp.float32, 0.0, math.log(10.0)))
    ramp = 1.0 + 2.0 * jnp.arange(D, dtype=jnp.float32)[None, :] / (D - 1)
    col_scale = ramp * jnp.exp(jax.random.uniform(key_cols, (1, D), jnp.float32, 0.0, math.log(10.0)))
    base = jnp.clip(jax.random.normal(key_base, (TOKENS, D), jnp.float32), -5.0, 5.0)
    return (base * row_scale * col_scale).astype(jnp.bfloat16)


def shared_keys(key):
    key_main = jax.random.fold_in(key, 31)
    values = jnp.clip(jax.random.normal(key_main, (D, KVH * HD), jnp.float32), -4.0, 4.0)
    return values / jnp.sqrt(jnp.float32(D))


def draw_k_weight(key, part):
    return shared_keys(key).astype(jnp.bfloat16)


def draw_q_weight(key, part):
    key_main = jax.random.fold_in(key, 21)
    values = jnp.clip(jax.random.normal(key_main, (D, QH * HD), jnp.float32), -4.0, 4.0)
    return (values / jnp.sqrt(jnp.float32(D))).astype(jnp.bfloat16)


def block_scale(rng, dims, cuts, least, high):
    def one(axis_at, blocks):
        draws = jax.random.uniform(jax.random.fold_in(jax.random.fold_in(rng, 6), axis_at), (blocks,), jnp.float32, least / len(cuts), high / len(cuts))
        return jnp.repeat(jnp.exp(draws), dims[axis_at] // blocks).reshape((-1,) + (1,) * (len(dims) - axis_at - 1))

    gain = one(*cuts[0])
    for cut in cuts[1:]:
        gain = gain * one(*cut)
    return gain


def normal_values(key, extent, deviation, bound, cuts=(), held_as=jnp.bfloat16):
    values = jax.random.normal(key, extent, jnp.float32) * deviation
    if len(cuts) > 0:
        values = block_scale(key, extent, cuts, -0.22, 0.18) * values
    return jnp.clip(values, min=-bound, max=bound).astype(held_as)


def setup_inputs(seed: int = 0) -> dict:
    splits = jax.random.split(jax.random.key(seed), 6)
    return {
        "hidden_in": draw_hidden_in(jax.random.fold_in(splits[5], 71), 0),
        "norm_gain": jnp.clip(1.0 + 0.18 * jax.random.normal(splits[1], (D,), jnp.float32), 0.099609375, 1.8984375).astype(jnp.bfloat16),
        "q_weight": draw_q_weight(jax.random.fold_in(splits[5], 71), 0),
        "k_weight": draw_k_weight(jax.random.fold_in(splits[5], 71), 0),
        "v_weight": normal_values(splits[4], (D, KVH * HD), D ** -0.5, 0.0625, ((0, 512),)),
    }


def rotate(field):
    half = field.shape[-1] // 2
    position = jnp.arange(field.shape[1], dtype=jnp.float32)
    freqs = 500000.0 ** (-(jnp.arange(half, dtype=jnp.float32) * 2.0) / field.shape[-1])
    angles = position[:, None] * freqs[None, :]
    cosine = jnp.cos(angles)[None, :, None, :]
    sine = jnp.sin(angles)[None, :, None, :]
    first = field[..., :half]
    second = field[..., half:]
    return jnp.concatenate([first * cosine - second * sine, second * cosine + first * sine], axis=-1)

def reference(hidden_in, norm_gain, q_weight, k_weight, v_weight):
    values = hidden_in.astype(jnp.float32)
    meansq = lax.optimization_barrier(jnp.mean(values * values, axis=-1, keepdims=True))
    normed = (values * lax.rsqrt(meansq + 1e-05) * norm_gain.astype(jnp.float32)).astype(jnp.bfloat16)
    q_lin = jnp.dot(normed, q_weight, preferred_element_type=jnp.float32)
    k_lin = jnp.dot(normed, k_weight, preferred_element_type=jnp.float32)
    v_lin = jnp.dot(normed, v_weight, preferred_element_type=jnp.float32)
    q_rot = rotate(q_lin.reshape(-1, SEQ, QH, HD)).astype(jnp.bfloat16)
    k_rot = rotate(k_lin.reshape(-1, SEQ, KVH, HD)).astype(jnp.bfloat16)
    v_all = v_lin.astype(jnp.bfloat16).reshape(-1, SEQ, KVH, HD)
    group = QH // KVH
    causal = jnp.tril(jnp.ones((SEQ, SEQ), dtype=bool))

    def attend(items):
        queries, keys, vals = items
        keys_wide = jnp.repeat(keys, group, axis=1).astype(jnp.float32)
        vals_wide = jnp.repeat(vals, group, axis=1).astype(jnp.float32)
        scores = jnp.einsum('shd,thd->hst', queries.astype(jnp.float32), keys_wide) / jnp.sqrt(jnp.float32(HD))
        scores = jnp.where(causal[None], scores, jnp.float32(-1e+30))
        top = lax.optimization_barrier(jnp.max(scores, axis=-1, keepdims=True))
        expo = jnp.exp(scores - top)
        probs = (expo / lax.optimization_barrier(jnp.sum(expo, axis=-1, keepdims=True))).astype(jnp.bfloat16)
        result = jnp.einsum('hst,thd->shd', probs.astype(jnp.float32), vals_wide)
        return result.astype(jnp.bfloat16).reshape(SEQ, QH * HD)
    outputs = lax.map(attend, (q_rot, k_rot, v_all))
    return outputs.reshape(-1, QH * HD)
```

```python
import functools

import jax
import jax.numpy as jnp
import numpy as np
from jax import lax
from jax.experimental import pallas as pl
from jax.experimental.pallas import tpu as pltpu
from jax.sharding import PartitionSpec as P

MESH = pl.DeviceIdType.MESH
BF16 = jnp.bfloat16
F32 = jnp.float32
HD = 128
SEQ = 512
ROWS = 128
CHUNKS = SEQ // ROWS
BLK = 512
D = 8192
SCALE = 1.0 / float(np.sqrt(np.float32(HD)))


def tables():
    position = np.arange(SEQ, dtype=np.float32)
    half = HD // 2
    freqs = np.power(np.float32(500000.0), -(np.arange(half, dtype=np.float32) * np.float32(2.0)) / np.float32(HD))
    angles = (position[:, None] * freqs[None, :].astype(np.float32)).astype(np.float32).astype(np.float64)
    cosine = np.cos(angles).astype(np.float32)
    sine = np.sin(angles).astype(np.float32)
    return np.concatenate([cosine, cosine], axis=1), np.concatenate([-sine, sine], axis=1)


def remote(src, dst, send, recv, device):
    return pltpu.make_async_remote_copy(
        src_ref=src, dst_ref=dst, send_sem=send, recv_sem=recv, device_id=device, device_id_type=MESH
    )


def kernel(
    hid, gain, qw, kw, vw, cos, sin, out,
    Z, W, H, R, S1, S2, PO, SB, RB, KB, VB,
    zr, zs, xr, xs, w1s, s1r, s1s, s2r, s2s, rr, rs, opr, ops, hr, hs_, hfr, hfs, er, es,
):
    b = lax.axis_index("batch")
    t = lax.axis_index("tensor")
    x, l = b // 8, b % 8
    y, h, c = t // 4, (t // 2) % 2, t % 2
    z = 8 * h + l
    oc = 1 - c

    def dev(xx, yy, zz, cc):
        return (8 * xx + zz % 8, 4 * yy + 2 * (zz // 8) + cc)

    xp, xm = (x + 1) % 4, (x + 3) % 4
    yp, ym, yo = (y + 1) % 4, (y + 3) % 4, (y + 2) % 4
    zp, zm = (z + 1) % 16, (z + 15) % 16
    z4p, z4m = (z + 4) % 16, (z + 12) % 16
    Dxp, Dxm = dev(xp, y, z, c), dev(xm, y, z, c)
    Dyp, Dym = dev(x, yp, z, c), dev(x, ym, z, c)
    Dzp, Dzm = dev(x, y, zp, c), dev(x, y, zm, c)
    D4p, D4m = dev(x, y, z4p, c), dev(x, y, z4m, c)
    Dpart = dev(x, y, z, oc)
    ring = [(yt, cc) for yt in (yp, ym, yo) for cc in (c, oc)] + [(y, oc)]

    barrier = pltpu.get_barrier_semaphore()
    peers = [Dxp, Dxm, Dzp, Dzm, D4p, D4m] + [dev(x, yt, z, cc) for yt, cc in ring]
    for peer in peers:
        pl.semaphore_signal(barrier, inc=1, device_id=peer, device_id_type=MESH)

    for r in range(CHUNKS):
        fold = None
        for g in range(4):
            v = hid[pl.ds(ROWS * r, ROWS), pl.ds(128 * g, 128)].astype(F32)
            fold = v * v if fold is None else fold + v * v
        S1[2 * y + c, :, pl.ds(ROWS * r, ROWS)] = jnp.sum(fold.T, axis=0, keepdims=True)

    pl.semaphore_wait(barrier, len(peers))

    cs = (l // 2) % 2
    lcz = 2 * (l // 4) + l % 2
    row0 = pl.multiple_of(16 * c, 16)

    def pieces(yt):
        a0 = pl.multiple_of(1024 * yt, 512)
        b0 = pl.multiple_of(128 * yt, 128)
        rows = pl.ds(row0, 16)
        return (
            (qw.at[:, pl.ds(a0, 512)], Z.at[lcz, y, h, rows, pl.ds(0, 512)]),
            (kw.at[:, pl.ds(b0, 128)], Z.at[lcz, y, h, rows, pl.ds(512, 128)]),
            (vw.at[:, pl.ds(b0, 128)], Z.at[lcz, y, h, rows, pl.ds(640, 128)]),
            (qw.at[:, pl.ds(pl.multiple_of(a0 + 512, 512), 512)], Z.at[lcz, y, h, rows, pl.ds(768, 512)]),
        )

    for i, yt in enumerate((yp, ym, yo)):
        for src, dst in pieces(yt):
            remote(src, dst, w1s.at[i], zr.at[lcz, h, y], dev(x, yt, z, cs)).start()

    @pl.when(cs == c)
    def _():
        for src, dst in pieces(y):
            pltpu.make_async_copy(src, dst, zr.at[lcz, h, y]).start()

    @pl.when(cs != c)
    def _():
        for src, dst in pieces(y):
            remote(src, dst, w1s.at[3], zr.at[lcz, h, y], Dpart).start()

    for i, (yt, cc) in enumerate(ring):
        remote(S1.at[2 * y + c], S1.at[2 * y + c], s1s.at[i], s1r.at[2 * y + c], dev(x, yt, z, cc)).start()

    col0 = pl.multiple_of(512 * h, 512)

    def slot(s):
        ls, hs = s % 8, s // 8
        return (ls // 2) % 2 == c, 2 * (ls // 4) + ls % 2, hs

    def zcopy(lc, hs, sub, d):
        ref = Z.at[lc, sub, hs]
        return remote(ref, ref, zs.at[d, lc, hs, sub], zr.at[lc, hs, sub], Dzp if d == 0 else Dzm)

    def xcopy(lc, hs, sub, d):
        return remote(
            Z.at[lc, sub, hs, :, pl.ds(col0, 768)], W.at[x, lc, sub, hs], xs.at[d, lc, hs, sub], xr.at[d, lc, hs, sub],
            Dxp if d == 0 else Dxm,
        )

    def xfcopy(lc, hs, sub, d):
        ref = W.at[xm if d == 0 else xp, lc, sub, hs]
        return remote(ref, ref, xs.at[2, lc, hs, sub], xr.at[2, lc, hs, sub], Dxp if d == 0 else Dxm)

    def process(s, dirs):
        mine, lc, hs = slot(s)

        @pl.when(mine)
        def _():
            def body(sub, carry):
                zcopy(lc, hs, sub, 0).wait_recv()
                for d in dirs:
                    zcopy(lc, hs, sub, d).start()
                for d in (0, 1):
                    xcopy(lc, hs, sub, d).start()
                return carry

            lax.fori_loop(0, 4, body, 0)

    def xforward(s):
        mine, lc, hs = slot(s)

        @pl.when(mine)
        def _():
            def body(i, carry):
                xcopy(lc, hs, i, 0).wait_recv()
                xfcopy(lc, hs, i, 0).start()
                xcopy(lc, hs, i + 2, 1).wait_recv()
                xfcopy(lc, hs, i + 2, 1).start()
                return carry

            lax.fori_loop(0, 2, body, 0)

    def zround(k):
        process((z + 16 - k) % 16, (0,) if k < 8 else ())
        if k < 8:
            process((z + k) % 16, (1,) if k < 7 else ())

    def xround(k):
        xforward((z + 16 - k) % 16)
        if 0 < k < 8:
            xforward((z + k) % 16)

    def hcopy(cls, r, d):
        hh = h if cls == 0 else 1 - h
        ref = H.at[y, hh, r]
        return remote(ref, ref, hs_.at[cls, d, r], hr.at[cls, d, r], Dyp if d == 0 else Dym)

    def hfcopy(cls, r):
        hh = h if cls == 0 else 1 - h
        ref = H.at[ym if r % 2 == 0 else yp, hh, r]
        return remote(ref, ref, hfs.at[cls, r], hfr.at[cls, r], Dyp if r % 2 == 0 else Dym)

    def leg1(r):
        return remote(H.at[y, h, r], R.at[r], rs.at[r], rr.at[r], D4p if r % 2 == 0 else D4m)

    def leg2(r):
        origin = z4m if r % 2 == 0 else z4p
        return remote(R.at[r], H.at[y, origin // 8, r], ops.at[r], opr.at[r], D4p if r % 2 == 0 else D4m)

    def relay(r):
        leg1(r).wait_recv()
        leg2(r).start()

    def spread(cls, r):
        hcopy(cls, r, 0).start()
        hcopy(cls, r, 1).start()

    def opposite(r):
        leg2(r).wait_recv()
        spread(1, r)

    def yforward(cls, r):
        hcopy(cls, r, r % 2).wait_recv()
        hfcopy(cls, r).start()

    def yfinish(cls, r):
        hcopy(cls, r, 1 - r % 2).wait_recv()
        hfcopy(cls, r).wait_recv()

    def s2copy(i):
        return remote(S2.at[i], S2.at[i + 1], s2s.at[i], s2r.at[i], D4p)

    process(z, (0, 1))

    for yt, cc in ring:
        remote(S1.at[2 * yt + cc], S1.at[2 * yt + cc], s1s.at[0], s1r.at[2 * yt + cc], Dpart).wait_recv()
    part = S1[0]
    for i in range(1, 8):
        part = part + S1[i]
    S2[0] = part
    s2copy(0).start()

    zround(1)
    xround(0)
    s2copy(0).wait_recv()
    s2copy(1).start()
    zround(2)
    xround(1)
    s2copy(1).wait_recv()
    total = S2[0] + S2[2]
    for r in range(CHUNKS):
        wide = jnp.broadcast_to(total[:, ROWS * r : ROWS * (r + 1)], (ROWS, ROWS)).T
        inv = lax.rsqrt(wide / D + 1e-05)
        for g in range(4):
            v = hid[pl.ds(ROWS * r, ROWS), pl.ds(128 * g, 128)].astype(F32)
            H[y, h, r, :, pl.ds(128 * g, 128)] = (v * inv * gain[:, pl.ds(128 * g, 128)].astype(F32)).astype(BF16)
        leg1(r).start()
        spread(0, r)

    zround(3)
    xround(2)
    yforward(0, 0)
    yforward(0, 1)
    zround(4)
    xround(3)
    yforward(0, 2)
    yforward(0, 3)
    relay(0)
    relay(1)
    zround(5)
    xround(4)
    zround(6)
    xround(5)
    relay(2)
    relay(3)
    zround(7)
    xround(6)
    opposite(0)
    opposite(1)
    zround(8)
    xround(7)
    yforward(1, 0)
    yforward(1, 1)
    xround(8)

    def wfinish(i, carry):
        lc, hs = i // 2, i % 2
        for sub in range(4):
            if sub < 2:
                xcopy(lc, hs, sub, 1).wait_recv()
            else:
                xcopy(lc, hs, sub, 0).wait_recv()
            xfcopy(lc, hs, sub, 0).wait_recv()
        return carry

    lax.fori_loop(0, 8, wfinish, 0)

    off_own = 256 * h + 256 * c
    off_oth = 256 * h + 256 * oc
    off_kv = 512 * (1 - h)

    def group(r, off):
        acc = None
        for rel in range(4):
            yb = (x + rel) % 4
            lhs = jnp.concatenate([H[yb, 0, r], H[yb, 1, r]], axis=1)
            if rel == 0:
                rhs = Z[:, :, :, :, pl.ds(pl.multiple_of(512 * h + off, 256), 256)]
            else:
                rhs = W[yb, :, :, :, :, pl.ds(pl.multiple_of(off, 256), 256)]
            prod = jnp.dot(lhs, rhs.reshape(1024, 256), preferred_element_type=F32)
            acc = prod if acc is None else acc + prod
        return acc

    def ecopy(r):
        return remote(SB.at[r], RB.at[r], es.at[r], er.at[r], Dpart)

    def project(r):
        yfinish(0, r)
        yfinish(1, r)
        SB[r, :, pl.ds(0, 256)] = group(r, off_oth)
        kv = group(r, off_kv)
        SB[r, :, pl.ds(256, 256)] = kv
        ecopy(r).start()
        PO[r, :, pl.ds(256, 256)] = kv
        PO[r, :, pl.ds(0, 256)] = group(r, off_own)

    def rotated(v, r):
        co = cos[pl.ds(ROWS * r, ROWS), :]
        si = sin[pl.ds(ROWS * r, ROWS), :]
        return (v * co + pltpu.roll(v, 64, 1) * si).astype(BF16)

    def attend(r):
        ecopy(r).wait_recv()

        def summed(j):
            return PO[r, :, pl.ds(128 * j, 128)] + RB[r, :, pl.ds(128 * j, 128)]

        KB[pl.ds(ROWS * r, ROWS), :] = rotated(summed(2), r)
        VB[pl.ds(ROWS * r, ROWS), :] = summed(3).astype(BF16)
        n = ROWS * (r + 1)
        keys = KB[pl.ds(0, n), :]
        vals = VB[pl.ds(0, n), :]
        row = lax.broadcasted_iota(jnp.int32, (ROWS, n), 0) + ROWS * r
        col = lax.broadcasted_iota(jnp.int32, (ROWS, n), 1)
        for j in range(2):
            query = rotated(summed(j), r)
            sc = lax.dot_general(query, keys, (((1,), (1,)), ((), ())), preferred_element_type=F32) * SCALE
            sc = jnp.where(col <= row, sc, F32(-1e30))
            top = jnp.max(sc, axis=1, keepdims=True)
            ex = jnp.exp(sc - top)
            probs = (ex / jnp.sum(ex, axis=1, keepdims=True)).astype(BF16)
            out[pl.ds(ROWS * r, ROWS), pl.ds(HD * j, HD)] = jnp.dot(probs, vals, preferred_element_type=F32).astype(BF16)

    project(0)
    project(1)
    opposite(2)
    opposite(3)
    attend(0)
    yforward(1, 2)
    yforward(1, 3)
    attend(1)
    project(2)
    project(3)
    attend(2)
    attend(3)

    for i, yt in enumerate((yp, ym, yo)):
        ref = Z.at[0, 0, 0, pl.ds(0, 16)]
        remote(ref, ref, w1s.at[i], s1r.at[0], Dpart).wait_send()

    @pl.when(cs != c)
    def _():
        ref = Z.at[0, 0, 0, pl.ds(0, 16)]
        remote(ref, ref, w1s.at[3], s1r.at[0], Dpart).wait_send()

    for i in range(7):
        remote(S1.at[0], S1.at[0], s1s.at[i], s1r.at[0], Dpart).wait_send()
    for i in range(2):
        s2copy(i).wait_send()

    def zdone(k, carry):
        mine, lc, hs = slot((z + 16 - k) % 16)

        @pl.when(mine)
        def _():
            for sub in range(4):
                zcopy(lc, hs, sub, 0).wait_send()

        return carry

    lax.fori_loop(0, 8, zdone, 0)

    def zdone_down(k, carry):
        mine, lc, hs = slot((z + k) % 16)

        @pl.when(mine)
        def _():
            for sub in range(4):
                zcopy(lc, hs, sub, 1).wait_send()

        return carry

    lax.fori_loop(0, 7, zdone_down, 0)

    def xdone(i, carry):
        lc, hs = i // 2, i % 2
        for sub in range(4):
            xcopy(lc, hs, sub, 0).wait_send()
            xcopy(lc, hs, sub, 1).wait_send()
            xfcopy(lc, hs, sub, 0).wait_send()
        return carry

    lax.fori_loop(0, 8, xdone, 0)
    for r in range(CHUNKS):
        leg1(r).wait_send()
        leg2(r).wait_send()
        ecopy(r).wait_send()
        for cls in (0, 1):
            hcopy(cls, r, 0).wait_send()
            hcopy(cls, r, 1).wait_send()
            hfcopy(cls, r).wait_send()


def on_device(hidden_in, norm_gain, q_weight, k_weight, v_weight):
    cos, sin = tables()
    dma = pltpu.SemaphoreType.DMA
    vmem = pltpu.VMEM
    return pl.pallas_call(
        kernel,
        out_shape=jax.ShapeDtypeStruct((SEQ, 256), BF16),
        in_specs=[pl.BlockSpec(memory_space=pltpu.VMEM)] * 7,
        out_specs=pl.BlockSpec(memory_space=pltpu.VMEM),
        scratch_shapes=[
            vmem((4, 4, 2, 32, 1280), BF16),
            vmem((4, 4, 4, 2, 32, 768), BF16),
            vmem((4, 2, CHUNKS, ROWS, BLK), BF16),
            vmem((CHUNKS, ROWS, BLK), BF16),
            vmem((8, 1, SEQ), F32),
            vmem((3, 1, SEQ), F32),
            vmem((CHUNKS, ROWS, 512), F32),
            vmem((CHUNKS, ROWS, 512), F32),
            vmem((CHUNKS, ROWS, 512), F32),
            vmem((SEQ, HD), BF16),
            vmem((SEQ, HD), BF16),
            dma((4, 2, 4)),
            dma((2, 4, 2, 4)),
            dma((3, 4, 2, 4)),
            dma((3, 4, 2, 4)),
            dma((4,)),
            dma((8,)),
            dma((7,)),
            dma((2,)),
            dma((2,)),
            dma((CHUNKS,)),
            dma((CHUNKS,)),
            dma((CHUNKS,)),
            dma((CHUNKS,)),
            dma((2, 2, CHUNKS)),
            dma((2, 2, CHUNKS)),
            dma((2, CHUNKS)),
            dma((2, CHUNKS)),
            dma((CHUNKS,)),
            dma((CHUNKS,)),
        ],
        compiler_params=pltpu.CompilerParams(
            collective_id=0, has_side_effects=True, vmem_limit_bytes=48 * 1024 * 1024
        ),
    )(hidden_in, norm_gain.reshape(1, -1), q_weight, k_weight, v_weight, jnp.asarray(cos), jnp.asarray(sin))


def solution(mesh):
    placed = (
        P("batch", "tensor"),
        P("tensor"),
        P(("batch", "tensor"), None),
        P(("batch", "tensor"), None),
        P(("batch", "tensor"), None),
    )
    return jax.shard_map(
        on_device, mesh=mesh, in_specs=placed, out_specs=P("batch", "tensor"), check_vma=False
    )
```

```python
import functools

import jax
import jax.numpy as jnp
import numpy as np
from jax import lax
from jax.experimental import pallas as pl
from jax.experimental.pallas import tpu as pltpu
from jax.sharding import PartitionSpec as P

MESH = pl.DeviceIdType.MESH
BF16 = jnp.bfloat16
F32 = jnp.float32
HD = 128
SEQ = 512
ROWS = 128
CHUNKS = SEQ // ROWS
BLK = 512
D = 8192
PIECE = 32
PER = ROWS // PIECE
SCHEDULE = (
    ('y',),
    ('z', 0),
    ('t',),
    ('h',),
    ('z', 1),
    ('z', 2),
    ('x', 0),
    ('z', 3),
    ('z', 4),
    ('x', 1),
    ('z', 5),
    ('x', 2),
    ('z', 6),
    ('x', 3),
    ('z', 7),
    ('z', 8),
    ('x', 4),
    ('s', 0, 16),
    ('x', 5),
    ('x', 6),
    ('o', 0, 1),
    ('x', 7),
    ('o', 1, 3),
    ('x', 8),
    ('o', 3, 6),
    ('f',),
    ('n',),
    ('o', 6, 9),
    ('p', 0),
    ('o', 9, 10),
    ('a', 0),
    ('o', 10, 11),
    ('p', 1),
    ('o', 11, 12),
    ('a', 1),
    ('o', 12, 13),
    ('p', 2),
    ('o', 13, 14),
    ('a', 2),
    ('o', 14, 16),
    ('p', 3),
    ('a', 3),
)
SCALE = 1.0 / float(np.sqrt(np.float32(HD)))


def tables():
    position = np.arange(SEQ, dtype=np.float32)
    half = HD // 2
    freqs = np.power(np.float32(500000.0), -(np.arange(half, dtype=np.float32) * np.float32(2.0)) / np.float32(HD))
    angles = (position[:, None] * freqs[None, :].astype(np.float32)).astype(np.float32).astype(np.float64)
    cosine = np.cos(angles).astype(np.float32)
    sine = np.sin(angles).astype(np.float32)
    return np.concatenate([cosine, cosine], axis=1), np.concatenate([-sine, sine], axis=1)


def remote(src, dst, send, recv, device):
    return pltpu.make_async_remote_copy(
        src_ref=src, dst_ref=dst, send_sem=send, recv_sem=recv, device_id=device, device_id_type=MESH
    )


def kernel(
    hid_in, gain, qw, kw, vw, cos_in, sin_in, out,
    cos, sin, Z, W, H, HX, S1, ST, IV, NB, PO, SB, RB, KB, VB,
    ld, zr, zs, xr, xs, xfs, hx, w1s, s1r, s1s, s2r, s2s, opr, ops, hr, hs_, gr, gs, er, es, far,
):
    b = lax.axis_index("batch")
    t = lax.axis_index("tensor")
    x, l = b // 8, b % 8
    y, h, c = t // 4, (t // 2) % 2, t % 2
    z = 8 * h + l
    oc = 1 - c

    def dev(xx, yy, zz, cc):
        return (8 * xx + zz % 8, 4 * yy + 2 * (zz // 8) + cc)

    xp, xm = (x + 1) % 4, (x + 3) % 4
    yp, ym, yo = (y + 1) % 4, (y + 3) % 4, (y + 2) % 4
    zp, zm, zo = (z + 1) % 16, (z + 15) % 16, (z + 8) % 16
    z4p, z4m = (z + 4) % 16, (z + 12) % 16
    Dxp, Dxm = dev(xp, y, z, c), dev(xm, y, z, c)
    Dy = (dev(x, yp, z, c), dev(x, ym, z, c), dev(x, yo, z, c))
    Dzp, Dzm, Dzo = dev(x, y, zp, c), dev(x, y, zm, c), dev(x, y, zo, c)
    D4p, D4m = dev(x, y, z4p, c), dev(x, y, z4m, c)
    Dpart = dev(x, y, z, oc)
    ring = [(yt, cc) for yt in (yp, ym, yo) for cc in (c, oc)] + [(y, oc)]

    loads = [
        pltpu.make_async_copy(src, dst, ld.at[i])
        for i, (src, dst) in enumerate(
            [(hid_in.at[pl.ds(ROWS * r, ROWS)], H.at[y, h, r]) for r in range(CHUNKS)] + [(cos_in, cos), (sin_in, sin)]
        )
    ]
    for load in loads:
        load.start()

    barrier = pltpu.get_barrier_semaphore()
    peers = [Dzp, Dzm] + [dev(x, yt, z, cc) for yt, cc in ring]
    for cc in (c, oc):
        peers += [dev(xp, y, z, cc), dev(xm, y, z, cc), dev(x, y, z4p, cc), dev(x, y, z4m, cc)]
    for peer in peers:
        pl.semaphore_signal(barrier, inc=1, device_id=peer, device_id_type=MESH)

    S1[2 * y + c, 1] = gain[...].astype(F32)
    for r in range(CHUNKS):
        loads[r].wait()
        fold = None
        for g in range(4):
            v = H[y, h, r, :, pl.ds(128 * g, 128)].astype(F32)
            fold = v * v if fold is None else fold + v * v
        S1[2 * y + c, 0, :, pl.ds(ROWS * r, ROWS)] = jnp.sum(fold.T, axis=0, keepdims=True)

    pl.semaphore_wait(barrier, len(peers))
    pl.semaphore_signal(far, inc=1, device_id=D4m, device_id_type=MESH)

    row0 = pl.multiple_of(16 * c, 16)

    def pieces(yt):
        a0 = pl.multiple_of(1024 * yt, 512)
        b0 = pl.multiple_of(128 * yt, 128)
        rows = pl.ds(row0, 16)
        return (
            (qw.at[:, pl.ds(a0, 512)], Z.at[l, y, h, rows, pl.ds(0, 512)]),
            (kw.at[:, pl.ds(b0, 128)], Z.at[l, y, h, rows, pl.ds(512, 128)]),
            (vw.at[:, pl.ds(b0, 128)], Z.at[l, y, h, rows, pl.ds(640, 128)]),
            (qw.at[:, pl.ds(pl.multiple_of(a0 + 512, 512), 512)], Z.at[l, y, h, rows, pl.ds(768, 512)]),
        )

    for i, yt in enumerate((yp, ym, yo)):
        for src, dst in pieces(yt):
            remote(src, dst, w1s.at[i], zr.at[l, h, y], dev(x, yt, z, 0)).start()

    @pl.when(c == 0)
    def _():
        for src, dst in pieces(y):
            pltpu.make_async_copy(src, dst, zr.at[l, h, y]).start()

    @pl.when(c == 1)
    def _():
        for src, dst in pieces(y):
            remote(src, dst, w1s.at[3], zr.at[l, h, y], Dpart).start()

    for i, (yt, cc) in enumerate(ring):
        remote(S1.at[2 * y + c], S1.at[2 * y + c], s1s.at[i], s1r.at[2 * y + c], dev(x, yt, z, cc)).start()

    col0 = pl.multiple_of(512 * h, 512)

    def slot(s):
        ls, hs = s % 8, s // 8
        return (ls // 2) % 2, 2 * (ls // 4) + ls % 2, hs

    def need(s, k, d):
        sl, hs = s % 8, s // 8
        if d == 0:
            return sl + k < 8, 1 - hs
        return jnp.logical_and(k <= sl, sl != 7), jnp.where(sl == 7, hs, 1 - hs)

    def zeach(s, k, d, sub, act):
        ls, hs = s % 8, s // 8
        both, half = need(s, k, d)
        sems = (zs.at[d, ls, hs, sub], zr.at[ls, hs, sub], Dzp if d == 0 else Dzm)

        @pl.when(both)
        def _():
            ref = Z.at[ls, sub, hs]
            act(remote(ref, ref, *sems))

        @pl.when(jnp.logical_not(both))
        def _():
            ref = Z.at[ls, sub, hs, :, pl.ds(pl.multiple_of(512 * half, 512), 768)]
            act(remote(ref, ref, *sems))

    def start(copy):
        copy.start()

    def wait_recv(copy):
        copy.wait_recv()

    def wait_send(copy):
        copy.wait_send()

    def xcopy(s, sub, d):
        cc, lc, hs = slot(s)
        ls = s % 8
        return remote(
            Z.at[ls, sub, hs, :, pl.ds(col0, 768)], W.at[x, lc, sub, hs], xs.at[d, ls, hs, sub], xr.at[d, lc, hs, sub],
            dev((xp, xm, x)[d], y, z, cc),
        )

    def xfcopy(lc, hs, sub, d):
        ref = W.at[xm if d == 0 else xp, lc, sub, hs]
        return remote(ref, ref, xfs.at[lc, hs, sub], xr.at[3, lc, hs, sub], Dxp if d == 0 else Dxm)

    def zstep(k, d, sub):
        s = (z + 16 - k) % 16 if d == 0 else (z + k) % 16
        cc, lc, hs = slot(s)
        if k == 0:
            ref = Z.at[s % 8, sub, hs]
            remote(ref, ref, zs.at[0, s % 8, hs, sub], zr.at[s % 8, hs, sub], Dzp).wait_recv()
            zeach(s, 1, 0, sub, start)
            zeach(s, 1, 1, sub, start)
        else:
            zeach(s, k, d, sub, wait_recv)
            if k < 8 - d:
                zeach(s, k + 1, d, sub, start)
        xcopy(s, sub, 0).start()
        xcopy(s, sub, 1).start()

        @pl.when(cc == 1)
        def _():
            xcopy(s, sub, 2).start()

        @pl.when(cc == 0)
        def _():
            pltpu.make_async_copy(
                Z.at[s % 8, sub, hs, :, pl.ds(col0, 768)], W.at[x, lc, sub, hs], xr.at[2, lc, hs, sub]
            ).start()

    def xstep(k, d, sub, way):
        s = (z + 16 - k) % 16 if d == 0 else (z + k) % 16
        cc, lc, hs = slot(s)

        @pl.when(cc == c)
        def _():
            xcopy(s, sub, way).wait_recv()
            xfcopy(lc, hs, sub, way).start()

    def zround(k):
        @pl.when(c == 0)
        def _():
            def body(sub, carry):
                zstep(k, 0, sub)
                if 0 < k < 8:
                    zstep(k, 1, sub)
                return carry

            lax.fori_loop(0, 4, body, 0)

    def xround(k):
        def body(i, carry):
            for j in range(2):
                xstep(k, 0, 2 * i + j, j)
                if 0 < k < 8:
                    xstep(k, 1, 2 * i + j, j)
            return carry

        lax.fori_loop(0, 2, body, 0)

    def hcopy(r, d):
        ref = H.at[y, h, r]
        return remote(ref, ref, hs_.at[d, r], hr.at[d, r], Dy[d])

    def hwait(r, d):
        hcopy(r, d).wait_recv()

    def ocopy(p, cc):
        part = (p // PER, pl.ds(PIECE * (p % PER), PIECE))
        src = H.at[y, h, part[0], part[1]] if cc == 1 else HX.at[part[0], part[1]]
        return remote(src, H.at[y, h, part[0], part[1]], ops.at[cc, p], opr.at[p], dev(x, y, zo, cc))

    pushed = remote(H.at[y, h], HX, hx.at[0], hx.at[1], Dpart)

    def push():
        @pl.when(c == 0)
        def _():
            pushed.start()

        @pl.when(c == 1)
        def _():
            pushed.wait_recv()

    def across(first, last):
        @pl.when(c == 1)
        def _():
            def body(p, carry):
                ocopy(p, 1).start()
                ocopy(p, 0).start()
                return carry

            lax.fori_loop(first, last, body, 0)

    def gcopy(p, d):
        ref = H.at[y, 1 - h, p // PER, pl.ds(PIECE * (p % PER), PIECE)]
        return remote(ref, ref, gs.at[d, p], gr.at[d, p], Dy[d])

    def opposite(p):
        ocopy(p, 1).wait_recv()
        for d in range(3):
            gcopy(p, d).start()

    s2copy = remote(ST.at[0], ST.at[1], s2s.at[0], s2r.at[0], Dzo)

    def stats():
        for yt, cc in ring:
            remote(S1.at[2 * yt + cc], S1.at[2 * yt + cc], s1s.at[0], s1r.at[2 * yt + cc], Dpart).wait_recv()
        part = S1[0, 0]
        for i in range(1, 8):
            part = part + S1[i, 0]
        ST[0, 0] = part
        for i in range(4):
            ST[0, 1 + i] = S1[2 * i + c, 1]
        pl.semaphore_wait(far, 1)
        s2copy.start()

    def scales():
        s2copy.wait_recv()
        total = ST[0, 0] + ST[1, 0]
        for r in range(CHUNKS):
            wide = jnp.broadcast_to(total[:, ROWS * r : ROWS * (r + 1)], (ROWS, ROWS)).T
            IV[r] = lax.rsqrt(wide / D + 1e-05)

    def normalize(r):
        for rel in range(4):
            yb = (x + rel) % 4
            for hb in range(2):
                own = jnp.where(h == hb, 0, 1)
                for g in range(4):
                    v = H[yb, hb, r, :, pl.ds(128 * g, 128)].astype(F32)
                    scale = ST[own, 1 + yb, :, pl.ds(128 * g, 128)]
                    NB[:, pl.ds(1024 * rel + 512 * hb + 128 * g, 128)] = (v * IV[r] * scale).astype(BF16)

    off_own = 256 * h + 256 * c
    off_oth = 256 * h + 256 * oc
    off_kv = 512 * (1 - h)

    def group(r, off):
        acc = None
        for rel in range(4):
            yb = (x + rel) % 4
            lhs = NB[:, pl.ds(1024 * rel, 1024)]
            rhs = W[yb, :, :, :, :, pl.ds(pl.multiple_of(off, 256), 256)]
            prod = jnp.dot(lhs, rhs.reshape(1024, 256), preferred_element_type=F32)
            acc = prod if acc is None else acc + prod
        return acc

    def ecopy(r):
        return remote(SB.at[r], RB.at[r], es.at[r], er.at[r], Dpart)

    def project(r):
        for d in range(3):
            hwait(r, d)
            for p in range(PER * r, PER * (r + 1)):
                gcopy(p, d).wait_recv()
        normalize(r)
        SB[r, :, pl.ds(0, 256)] = group(r, off_oth)
        kv = group(r, off_kv)
        SB[r, :, pl.ds(256, 256)] = kv
        ecopy(r).start()
        PO[r, :, pl.ds(256, 256)] = kv
        PO[r, :, pl.ds(0, 256)] = group(r, off_own)

    def rotated(v, r):
        co = cos[pl.ds(ROWS * r, ROWS), :]
        si = sin[pl.ds(ROWS * r, ROWS), :]
        return (v * co + pltpu.roll(v, 64, 1) * si).astype(BF16)

    def attend(r):
        ecopy(r).wait_recv()

        def summed(j):
            return PO[r, :, pl.ds(128 * j, 128)] + RB[r, :, pl.ds(128 * j, 128)]

        KB[pl.ds(ROWS * r, ROWS), :] = rotated(summed(2), r)
        VB[pl.ds(ROWS * r, ROWS), :] = summed(3).astype(BF16)
        n = ROWS * (r + 1)
        keys = KB[pl.ds(0, n), :]
        vals = VB[pl.ds(0, n), :]
        row = lax.broadcasted_iota(jnp.int32, (ROWS, n), 0) + ROWS * r
        col = lax.broadcasted_iota(jnp.int32, (ROWS, n), 1)
        for j in range(2):
            query = rotated(summed(j), r)
            sc = lax.dot_general(query, keys, (((1,), (1,)), ((), ())), preferred_element_type=F32) * SCALE
            sc = jnp.where(col <= row, sc, F32(-1e30))
            top = jnp.max(sc, axis=1, keepdims=True)
            ex = jnp.exp(sc - top)
            probs = (ex / jnp.sum(ex, axis=1, keepdims=True)).astype(BF16)
            out[pl.ds(ROWS * r, ROWS), pl.ds(HD * j, HD)] = jnp.dot(probs, vals, preferred_element_type=F32).astype(BF16)

    def wfinish():
        def body(i, carry):
            lc, hs = i // 2, i % 2
            for sub in range(4):
                source = 8 * hs + 4 * (lc // 2) + 2 * c + lc % 2
                xcopy(source, sub, 1 - sub % 2).wait_recv()
                xcopy(source, sub, 2).wait_recv()
                xfcopy(lc, hs, sub, 0).wait_recv()
            return carry

        lax.fori_loop(0, 8, body, 0)

    def rope_tables():
        loads[CHUNKS].wait()
        loads[CHUNKS + 1].wait()

    for step in SCHEDULE:
        name, args = step[0], step[1:]
        if name == "z":
            zround(*args)
        elif name == "x":
            xround(*args)
        elif name == "t":
            stats()
        elif name == "n":
            scales()
        elif name == "y":
            for r in range(CHUNKS):
                for d in range(3):
                    hcopy(r, d).start()
        elif name == "h":
            push()
        elif name == "s":
            across(*args)
        elif name == "o":
            for p in range(*args):
                opposite(p)
        elif name == "f":
            wfinish()
            rope_tables()
        elif name == "p":
            project(*args)
        else:
            attend(*args)

    piece16 = Z.at[0, 0, 0, pl.ds(0, 16)]
    for i in range(3):
        remote(piece16, piece16, w1s.at[i], s1r.at[0], Dpart).wait_send()

    @pl.when(c == 1)
    def _():
        remote(piece16, piece16, w1s.at[3], s1r.at[0], Dpart).wait_send()

    for i in range(7):
        remote(S1.at[0], S1.at[0], s1s.at[i], s1r.at[0], Dpart).wait_send()
    s2copy.wait_send()

    def zdone(d):
        def body(k, carry):
            s = (z + 16 - k) % 16 if d == 0 else (z + k) % 16
            for sub in range(4):
                zeach(s, k + 1, d, sub, wait_send)
            return carry

        lax.fori_loop(0, 8 - d, body, 0)

    @pl.when(c == 0)
    def _():
        pushed.wait_send()
        zdone(0)
        zdone(1)

        def xdone(s, carry):
            for sub in range(4):
                xcopy(s, sub, 0).wait_send()
                xcopy(s, sub, 1).wait_send()

                @pl.when(slot(s)[0] == 1)
                def _():
                    xcopy(s, sub, 2).wait_send()

            return carry

        lax.fori_loop(0, 16, xdone, 0)

    def xfdone(i, carry):
        for sub in range(4):
            xfcopy(i // 2, i % 2, sub, 0).wait_send()
        return carry

    lax.fori_loop(0, 8, xfdone, 0)
    for r in range(CHUNKS):
        ecopy(r).wait_send()
        for d in range(3):
            hcopy(r, d).wait_send()

    def pdone(p, carry):
        @pl.when(c == 1)
        def _():
            ocopy(p, 0).wait_send()
            ocopy(p, 1).wait_send()

        for d in range(3):
            gcopy(p, d).wait_send()
        return carry

    lax.fori_loop(0, PER * CHUNKS, pdone, 0)


def on_device(hidden_in, norm_gain, q_weight, k_weight, v_weight):
    cos, sin = tables()
    dma = pltpu.SemaphoreType.DMA
    vmem = pltpu.VMEM
    hbm = pl.BlockSpec(memory_space=pltpu.HBM)
    return pl.pallas_call(
        kernel,
        out_shape=jax.ShapeDtypeStruct((SEQ, 256), BF16),
        in_specs=[hbm, pl.BlockSpec(memory_space=vmem), hbm, hbm, hbm, hbm, hbm],
        out_specs=pl.BlockSpec(memory_space=vmem),
        scratch_shapes=[
            vmem((SEQ, HD), F32),
            vmem((SEQ, HD), F32),
            vmem((8, 4, 2, 32, 1280), BF16),
            vmem((4, 4, 4, 2, 32, 768), BF16),
            vmem((4, 2, CHUNKS, ROWS, BLK), BF16),
            vmem((CHUNKS, ROWS, BLK), BF16),
            vmem((8, 2, 1, SEQ), F32),
            vmem((2, 5, 1, SEQ), F32),
            vmem((CHUNKS, ROWS, ROWS), F32),
            vmem((ROWS, 8 * BLK), BF16),
            vmem((CHUNKS, ROWS, 512), F32),
            vmem((CHUNKS, ROWS, 512), F32),
            vmem((CHUNKS, ROWS, 512), F32),
            vmem((SEQ, HD), BF16),
            vmem((SEQ, HD), BF16),
            dma((CHUNKS + 2,)),
            dma((8, 2, 4)),
            dma((2, 8, 2, 4)),
            dma((4, 4, 2, 4)),
            dma((3, 8, 2, 4)),
            dma((4, 2, 4)),
            dma((2,)),
            dma((4,)),
            dma((8,)),
            dma((7,)),
            dma((1,)),
            dma((1,)),
            dma((PER * CHUNKS,)),
            dma((2, PER * CHUNKS)),
            dma((3, CHUNKS)),
            dma((3, CHUNKS)),
            dma((3, PER * CHUNKS)),
            dma((3, PER * CHUNKS)),
            dma((CHUNKS,)),
            dma((CHUNKS,)),
            pltpu.SemaphoreType.REGULAR,
        ],
        compiler_params=pltpu.CompilerParams(
            collective_id=0, has_side_effects=True, vmem_limit_bytes=67043328
        ),
    )(hidden_in, norm_gain.reshape(1, -1), q_weight, k_weight, v_weight, jnp.asarray(cos), jnp.asarray(sin))


def solution(mesh):
    placed = (
        P("batch", "tensor"),
        P("tensor"),
        P(("batch", "tensor"), None),
        P(("batch", "tensor"), None),
        P(("batch", "tensor"), None),
    )
    return jax.shard_map(
        on_device, mesh=mesh, in_specs=placed, out_specs=P("batch", "tensor"), check_vma=False
    )
```

```python
import functools

import jax
import jax.numpy as jnp
import numpy as np
from jax import lax
from jax.experimental import pallas as pl
from jax.experimental.pallas import tpu as pltpu
from jax.sharding import PartitionSpec as P

MESH = pl.DeviceIdType.MESH
BF16 = jnp.bfloat16
F32 = jnp.float32
HD = 128
SEQ = 512
ROWS = 128
CHUNKS = SEQ // ROWS
BLK = 512
D = 8192
PIECE = 32
PER = ROWS // PIECE
SCHEDULE = (
    ('y',),
    ('z', 0),
    ('t',),
    ('h',),
    ('z', 1),
    ('z', 2),
    ('x', 0),
    ('z', 3),
    ('z', 4),
    ('x', 1),
    ('z', 5),
    ('z', 6),
    ('x', 2),
    ('z', 7),
    ('z', 8),
    ('x', 3),
    ('x', 4),
    ('s', 0, 16),
    ('x', 5),
    ('x', 6),
    ('o', 0, 1),
    ('x', 7),
    ('o', 1, 3),
    ('x', 8),
    ('o', 3, 6),
    ('f',),
    ('n',),
    ('o', 6, 8),
    ('b', 0),
    ('o', 8, 9),
    ('b', 1),
    ('o', 9, 10),
    ('p', 0),
    ('a', 0),
    ('o', 10, 11),
    ('b', 2),
    ('o', 11, 12),
    ('p', 1),
    ('b', 3),
    ('o', 12, 13),
    ('a', 1),
    ('o', 13, 14),
    ('p', 2),
    ('o', 14, 15),
    ('a', 2),
    ('o', 15, 16),
    ('p', 3),
    ('a', 3),
)
SCALE = 1.0 / float(np.sqrt(np.float32(HD)))


def tables():
    position = np.arange(SEQ, dtype=np.float32)
    half = HD // 2
    freqs = np.power(np.float32(500000.0), -(np.arange(half, dtype=np.float32) * np.float32(2.0)) / np.float32(HD))
    angles = (position[:, None] * freqs[None, :].astype(np.float32)).astype(np.float32).astype(np.float64)
    cosine = np.cos(angles).astype(np.float32)
    sine = np.sin(angles).astype(np.float32)
    return np.concatenate([cosine, cosine], axis=1), np.concatenate([-sine, sine], axis=1)


def remote(src, dst, send, recv, device):
    return pltpu.make_async_remote_copy(
        src_ref=src, dst_ref=dst, send_sem=send, recv_sem=recv, device_id=device, device_id_type=MESH
    )


def kernel(
    hid_in, gain, qw, kw, vw, cos_in, sin_in, out,
    cos, sin, Z, W, H, HX, S1, ST, IV, NB, PO, SB, RB, KB, VB,
    ld, zr, zs, xr, xs, xfs, hx, w1s, s1r, s1s, s2r, s2s, opr, ops, hr, hs_, gr, gs, er, es, far,
):
    b = lax.axis_index("batch")
    t = lax.axis_index("tensor")
    x, l = b // 8, b % 8
    y, h, c = t // 4, (t // 2) % 2, t % 2
    z = 8 * h + l
    oc = 1 - c

    def dev(xx, yy, zz, cc):
        return (8 * xx + zz % 8, 4 * yy + 2 * (zz // 8) + cc)

    xp, xm = (x + 1) % 4, (x + 3) % 4
    yp, ym, yo = (y + 1) % 4, (y + 3) % 4, (y + 2) % 4
    zp, zm, zo = (z + 1) % 16, (z + 15) % 16, (z + 8) % 16
    z4p, z4m = (z + 4) % 16, (z + 12) % 16
    Dxp, Dxm = dev(xp, y, z, c), dev(xm, y, z, c)
    Dy = (dev(x, yp, z, c), dev(x, ym, z, c), dev(x, yo, z, c))
    Dzp, Dzm, Dzo = dev(x, y, zp, c), dev(x, y, zm, c), dev(x, y, zo, c)
    D4p, D4m = dev(x, y, z4p, c), dev(x, y, z4m, c)
    Dpart = dev(x, y, z, oc)
    ring = [(yt, cc) for yt in (yp, ym, yo) for cc in (c, oc)] + [(y, oc)]

    loads = [
        pltpu.make_async_copy(src, dst, ld.at[i])
        for i, (src, dst) in enumerate(
            [(hid_in.at[pl.ds(ROWS * r, ROWS)], H.at[y, h, r]) for r in range(CHUNKS)] + [(cos_in, cos), (sin_in, sin)]
        )
    ]
    for load in loads:
        load.start()

    barrier = pltpu.get_barrier_semaphore()
    peers = [Dzp, Dzm] + [dev(x, yt, z, cc) for yt, cc in ring]
    for cc in (c, oc):
        peers += [dev(xp, y, z, cc), dev(xm, y, z, cc), dev(x, y, z4p, cc), dev(x, y, z4m, cc)]
    for peer in peers:
        pl.semaphore_signal(barrier, inc=1, device_id=peer, device_id_type=MESH)

    S1[2 * y + c, 1] = gain[...].astype(F32).reshape(1, BLK)
    for r in range(CHUNKS):
        loads[r].wait()
        fold = None
        for g in range(4):
            v = H[y, h, r, :, pl.ds(128 * g, 128)].astype(F32)
            fold = v * v if fold is None else fold + v * v
        S1[2 * y + c, 0, :, pl.ds(ROWS * r, ROWS)] = jnp.sum(fold.T, axis=0, keepdims=True)

    pl.semaphore_wait(barrier, len(peers))
    pl.semaphore_signal(far, inc=1, device_id=D4m, device_id_type=MESH)

    row0 = pl.multiple_of(16 * c, 16)

    def pieces(yt):
        a0 = pl.multiple_of(1024 * yt, 512)
        b0 = pl.multiple_of(128 * yt, 128)
        rows = pl.ds(row0, 16)
        return (
            (qw.at[:, pl.ds(a0, 512)], Z.at[l, y, h, rows, pl.ds(0, 512)]),
            (kw.at[:, pl.ds(b0, 128)], Z.at[l, y, h, rows, pl.ds(512, 128)]),
            (vw.at[:, pl.ds(b0, 128)], Z.at[l, y, h, rows, pl.ds(640, 128)]),
            (qw.at[:, pl.ds(pl.multiple_of(a0 + 512, 512), 512)], Z.at[l, y, h, rows, pl.ds(768, 512)]),
        )

    for i, yt in enumerate((yp, ym, yo)):
        for src, dst in pieces(yt):
            remote(src, dst, w1s.at[i], zr.at[l, h, y], dev(x, yt, z, 0)).start()

    @pl.when(c == 0)
    def _():
        for src, dst in pieces(y):
            pltpu.make_async_copy(src, dst, zr.at[l, h, y]).start()

    @pl.when(c == 1)
    def _():
        for src, dst in pieces(y):
            remote(src, dst, w1s.at[3], zr.at[l, h, y], Dpart).start()

    for i, (yt, cc) in enumerate(ring):
        remote(S1.at[2 * y + c], S1.at[2 * y + c], s1s.at[i], s1r.at[2 * y + c], dev(x, yt, z, cc)).start()

    col0 = pl.multiple_of(512 * h, 512)

    def slot(s):
        ls, hs = s % 8, s // 8
        return (ls // 2) % 2, 2 * (ls // 4) + ls % 2, hs

    def need(s, k, d):
        sl, hs = s % 8, s // 8
        if d == 0:
            return sl + k < 8, 1 - hs
        return jnp.logical_and(k <= sl, sl != 7), jnp.where(sl == 7, hs, 1 - hs)

    def zeach(s, k, d, sub, act):
        ls, hs = s % 8, s // 8
        both, half = need(s, k, d)
        sems = (zs.at[d, ls, hs, sub], zr.at[ls, hs, sub], Dzp if d == 0 else Dzm)

        @pl.when(both)
        def _():
            ref = Z.at[ls, sub, hs]
            act(remote(ref, ref, *sems))

        @pl.when(jnp.logical_not(both))
        def _():
            ref = Z.at[ls, sub, hs, :, pl.ds(pl.multiple_of(512 * half, 512), 768)]
            act(remote(ref, ref, *sems))

    def start(copy):
        copy.start()

    def wait_recv(copy):
        copy.wait_recv()

    def wait_send(copy):
        copy.wait_send()

    def xcopy(s, sub, d):
        cc, lc, hs = slot(s)
        ls = s % 8
        return remote(
            Z.at[ls, sub, hs, :, pl.ds(col0, 768)], W.at[x, lc, sub, hs], xs.at[d, ls, hs, sub], xr.at[d, lc, hs, sub],
            dev((xp, xm, x)[d], y, z, cc),
        )

    def xfcopy(lc, hs, sub, d):
        ref = W.at[xm if d == 0 else xp, lc, sub, hs]
        return remote(ref, ref, xfs.at[lc, hs, sub], xr.at[3, lc, hs, sub], Dxp if d == 0 else Dxm)

    def zstep(k, d, sub):
        s = (z + 16 - k) % 16 if d == 0 else (z + k) % 16
        cc, lc, hs = slot(s)
        if k == 0:
            ref = Z.at[s % 8, sub, hs]
            remote(ref, ref, zs.at[0, s % 8, hs, sub], zr.at[s % 8, hs, sub], Dzp).wait_recv()
            zeach(s, 1, 0, sub, start)
            zeach(s, 1, 1, sub, start)
        else:
            zeach(s, k, d, sub, wait_recv)
            if k < 8 - d:
                zeach(s, k + 1, d, sub, start)
        xcopy(s, sub, 0).start()
        xcopy(s, sub, 1).start()

        @pl.when(cc == 1)
        def _():
            xcopy(s, sub, 2).start()

        @pl.when(cc == 0)
        def _():
            pltpu.make_async_copy(
                Z.at[s % 8, sub, hs, :, pl.ds(col0, 768)], W.at[x, lc, sub, hs], xr.at[2, lc, hs, sub]
            ).start()

    def xstep(k, d, sub, way):
        s = (z + 16 - k) % 16 if d == 0 else (z + k) % 16
        cc, lc, hs = slot(s)

        @pl.when(cc == c)
        def _():
            xcopy(s, sub, way).wait_recv()
            xfcopy(lc, hs, sub, way).start()

    def zround(k):
        @pl.when(c == 0)
        def _():
            def body(sub, carry):
                zstep(k, 0, sub)
                if 0 < k < 8:
                    zstep(k, 1, sub)
                return carry

            lax.fori_loop(0, 4, body, 0)

    def xround(k, first=0, last=2):
        def body(i, carry):
            for j in range(2):
                xstep(k, 0, 2 * i + j, j)
                if 0 < k < 8:
                    xstep(k, 1, 2 * i + j, j)
            return carry

        lax.fori_loop(first, last, body, 0)

    def hcopy(r, d):
        ref = H.at[y, h, r]
        return remote(ref, ref, hs_.at[d, r], hr.at[d, r], Dy[d])

    def hwait(r, d):
        hcopy(r, d).wait_recv()

    def ocopy(p, cc):
        part = (p // PER, pl.ds(PIECE * (p % PER), PIECE))
        src = H.at[y, h, part[0], part[1]] if cc == 1 else HX.at[part[0], part[1]]
        return remote(src, H.at[y, h, part[0], part[1]], ops.at[cc, p], opr.at[p], dev(x, y, zo, cc))

    pushed = remote(H.at[y, h], HX, hx.at[0], hx.at[1], Dpart)

    def push():
        @pl.when(c == 0)
        def _():
            pushed.start()

        @pl.when(c == 1)
        def _():
            pushed.wait_recv()

    def across(first, last):
        @pl.when(c == 1)
        def _():
            def body(p, carry):
                ocopy(p, 1).start()
                ocopy(p, 0).start()
                return carry

            lax.fori_loop(first, last, body, 0)

    def gcopy(p, d):
        ref = H.at[y, 1 - h, p // PER, pl.ds(PIECE * (p % PER), PIECE)]
        return remote(ref, ref, gs.at[d, p], gr.at[d, p], Dy[d])

    def opposite(p):
        ocopy(p, 1).wait_recv()
        for d in range(3):
            gcopy(p, d).start()

    s2copy = remote(ST.at[0], ST.at[1], s2s.at[0], s2r.at[0], Dzo)

    def stats():
        for yt, cc in ring:
            remote(S1.at[2 * yt + cc], S1.at[2 * yt + cc], s1s.at[0], s1r.at[2 * yt + cc], Dpart).wait_recv()
        part = S1[0, 0]
        for i in range(1, 8):
            part = part + S1[i, 0]
        ST[0, 0] = part
        for i in range(4):
            ST[0, 1 + i] = S1[2 * i + c, 1]
        pl.semaphore_wait(far, 1)
        s2copy.start()

    def scales():
        s2copy.wait_recv()
        total = ST[0, 0] + ST[1, 0]
        for r in range(CHUNKS):
            wide = jnp.broadcast_to(total[:, ROWS * r : ROWS * (r + 1)], (ROWS, ROWS)).T
            IV[r] = lax.rsqrt(wide / D + 1e-05)

    def normalize(r, hb, side):
        for rel in range(4):
            yb = (x + rel) % 4
            for g in range(4):
                v = H[yb, hb, r, :, pl.ds(128 * g, 128)].astype(F32)
                scale = ST[side, 1 + yb, :, pl.ds(128 * g, 128)]
                NB[:, pl.ds(512 * rel + 128 * g, 128)] = (v * IV[r] * scale).astype(BF16)

    off_own = 256 * h + 256 * c
    off_oth = 256 * h + 256 * oc
    off_kv = 512 * (1 - h)

    def group(hb, off):
        acc = None
        for rel in range(4):
            yb = (x + rel) % 4
            lhs = NB[:, pl.ds(512 * rel, 512)]
            rhs = W[yb, pl.ds(2 * hb, 2), :, :, :, pl.ds(pl.multiple_of(off, 256), 256)]
            prod = jnp.dot(lhs, rhs.reshape(512, 256), preferred_element_type=F32)
            acc = prod if acc is None else acc + prod
        return acc

    def ecopy(r):
        return remote(SB.at[r], RB.at[r], es.at[r], er.at[r], Dpart)

    def begin(r):
        for d in range(3):
            hwait(r, d)
        normalize(r, h, 0)
        SB[r, :, pl.ds(0, 256)] = group(h, off_oth)
        SB[r, :, pl.ds(256, 256)] = group(h, off_kv)
        PO[r, :, pl.ds(0, 256)] = group(h, off_own)

    def project(r):
        for d in range(3):
            for p in range(PER * r, PER * (r + 1)):
                gcopy(p, d).wait_recv()
        normalize(r, 1 - h, 1)
        SB[r, :, pl.ds(0, 256)] += group(1 - h, off_oth)
        kv = SB[r, :, pl.ds(256, 256)] + group(1 - h, off_kv)
        SB[r, :, pl.ds(256, 256)] = kv
        ecopy(r).start()
        PO[r, :, pl.ds(256, 256)] = kv
        PO[r, :, pl.ds(0, 256)] += group(1 - h, off_own)

    def rotated(v, r):
        co = cos[pl.ds(ROWS * r, ROWS), :]
        si = sin[pl.ds(ROWS * r, ROWS), :]
        return (v * co + pltpu.roll(v, 64, 1) * si).astype(BF16)

    def attend(r):
        ecopy(r).wait_recv()

        def summed(j):
            return PO[r, :, pl.ds(128 * j, 128)] + RB[r, :, pl.ds(128 * j, 128)]

        KB[pl.ds(ROWS * r, ROWS), :] = rotated(summed(2), r)
        VB[pl.ds(ROWS * r, ROWS), :] = summed(3).astype(BF16)
        n = ROWS * (r + 1)
        keys = KB[pl.ds(0, n), :]
        vals = VB[pl.ds(0, n), :]
        row = lax.broadcasted_iota(jnp.int32, (ROWS, n), 0) + ROWS * r
        col = lax.broadcasted_iota(jnp.int32, (ROWS, n), 1)
        for j in range(2):
            query = rotated(summed(j), r)
            sc = lax.dot_general(query, keys, (((1,), (1,)), ((), ())), preferred_element_type=F32) * SCALE
            sc = jnp.where(col <= row, sc, F32(-1e30))
            top = jnp.max(sc, axis=1, keepdims=True)
            ex = jnp.exp(sc - top)
            probs = (ex / jnp.sum(ex, axis=1, keepdims=True)).astype(BF16)
            out[pl.ds(ROWS * r, ROWS), pl.ds(HD * j, HD)] = jnp.dot(probs, vals, preferred_element_type=F32).astype(BF16)

    def wfinish():
        def body(i, carry):
            lc, hs = i // 2, i % 2
            for sub in range(4):
                source = 8 * hs + 4 * (lc // 2) + 2 * c + lc % 2
                xcopy(source, sub, 1 - sub % 2).wait_recv()
                xcopy(source, sub, 2).wait_recv()
                xfcopy(lc, hs, sub, 0).wait_recv()
            return carry

        lax.fori_loop(0, 8, body, 0)

    def rope_tables():
        loads[CHUNKS].wait()
        loads[CHUNKS + 1].wait()

    for step in SCHEDULE:
        name, args = step[0], step[1:]
        if name == "z":
            zround(*args)
        elif name == "x":
            xround(*args)
        elif name == "t":
            stats()
        elif name == "n":
            scales()
        elif name == "y":
            for r in range(CHUNKS):
                for d in range(3):
                    hcopy(r, d).start()
        elif name == "h":
            push()
        elif name == "s":
            across(*args)
        elif name == "o":
            for p in range(*args):
                opposite(p)
        elif name == "f":
            wfinish()
            rope_tables()
        elif name == "b":
            begin(*args)
        elif name == "p":
            project(*args)
        else:
            attend(*args)

    piece16 = Z.at[0, 0, 0, pl.ds(0, 16)]
    for i in range(3):
        remote(piece16, piece16, w1s.at[i], s1r.at[0], Dpart).wait_send()

    @pl.when(c == 1)
    def _():
        remote(piece16, piece16, w1s.at[3], s1r.at[0], Dpart).wait_send()

    for i in range(7):
        remote(S1.at[0], S1.at[0], s1s.at[i], s1r.at[0], Dpart).wait_send()
    s2copy.wait_send()

    def zdone(d):
        def body(k, carry):
            s = (z + 16 - k) % 16 if d == 0 else (z + k) % 16
            for sub in range(4):
                zeach(s, k + 1, d, sub, wait_send)
            return carry

        lax.fori_loop(0, 8 - d, body, 0)

    @pl.when(c == 0)
    def _():
        pushed.wait_send()
        zdone(0)
        zdone(1)

        def xdone(s, carry):
            for sub in range(4):
                xcopy(s, sub, 0).wait_send()
                xcopy(s, sub, 1).wait_send()

                @pl.when(slot(s)[0] == 1)
                def _():
                    xcopy(s, sub, 2).wait_send()

            return carry

        lax.fori_loop(0, 16, xdone, 0)

    def xfdone(i, carry):
        for sub in range(4):
            xfcopy(i // 2, i % 2, sub, 0).wait_send()
        return carry

    lax.fori_loop(0, 8, xfdone, 0)
    for r in range(CHUNKS):
        ecopy(r).wait_send()
        for d in range(3):
            hcopy(r, d).wait_send()

    def pdone(p, carry):
        @pl.when(c == 1)
        def _():
            ocopy(p, 0).wait_send()
            ocopy(p, 1).wait_send()

        for d in range(3):
            gcopy(p, d).wait_send()
        return carry

    lax.fori_loop(0, PER * CHUNKS, pdone, 0)


def on_device(hidden_in, norm_gain, q_weight, k_weight, v_weight):
    cos, sin = tables()
    dma = pltpu.SemaphoreType.DMA
    vmem = pltpu.VMEM
    hbm = pl.BlockSpec(memory_space=pltpu.HBM)
    return pl.pallas_call(
        kernel,
        out_shape=jax.ShapeDtypeStruct((SEQ, 256), BF16),
        in_specs=[hbm, pl.BlockSpec(memory_space=vmem), hbm, hbm, hbm, hbm, hbm],
        out_specs=pl.BlockSpec(memory_space=vmem),
        scratch_shapes=[
            vmem((SEQ, HD), F32),
            vmem((SEQ, HD), F32),
            vmem((8, 4, 2, 32, 1280), BF16),
            vmem((4, 4, 4, 2, 32, 768), BF16),
            vmem((4, 2, CHUNKS, ROWS, BLK), BF16),
            vmem((CHUNKS, ROWS, BLK), BF16),
            vmem((8, 2, 1, SEQ), F32),
            vmem((2, 5, 1, SEQ), F32),
            vmem((CHUNKS, ROWS, ROWS), F32),
            vmem((ROWS, 4 * BLK), BF16),
            vmem((CHUNKS, ROWS, 512), F32),
            vmem((CHUNKS, ROWS, 512), F32),
            vmem((CHUNKS, ROWS, 512), F32),
            vmem((SEQ, HD), BF16),
            vmem((SEQ, HD), BF16),
            dma((CHUNKS + 2,)),
            dma((8, 2, 4)),
            dma((2, 8, 2, 4)),
            dma((4, 4, 2, 4)),
            dma((3, 8, 2, 4)),
            dma((4, 2, 4)),
            dma((2,)),
            dma((4,)),
            dma((8,)),
            dma((7,)),
            dma((1,)),
            dma((1,)),
            dma((PER * CHUNKS,)),
            dma((2, PER * CHUNKS)),
            dma((3, CHUNKS)),
            dma((3, CHUNKS)),
            dma((3, PER * CHUNKS)),
            dma((3, PER * CHUNKS)),
            dma((CHUNKS,)),
            dma((CHUNKS,)),
            pltpu.SemaphoreType.REGULAR,
        ],
        compiler_params=pltpu.CompilerParams(
            collective_id=0, has_side_effects=True, vmem_limit_bytes=67043328
        ),
    )(hidden_in, norm_gain, q_weight, k_weight, v_weight, jnp.asarray(cos), jnp.asarray(sin))


def solution(mesh):
    placed = (
        P("batch", "tensor"),
        P("tensor"),
        P(("batch", "tensor"), None),
        P(("batch", "tensor"), None),
        P(("batch", "tensor"), None),
    )
    return jax.shard_map(
        on_device, mesh=mesh, in_specs=placed, out_specs=P("batch", "tensor"), check_vma=False
    )
```

```python
import functools

import jax
import jax.numpy as jnp
import numpy as np
from jax import lax
from jax.experimental import pallas as pl
from jax.experimental.pallas import tpu as pltpu
from jax.sharding import PartitionSpec as P

MESH = pl.DeviceIdType.MESH
BF16 = jnp.bfloat16
F32 = jnp.float32
HD = 128
SEQ = 512
ROWS = 128
CHUNKS = SEQ // ROWS
BLK = 512
D = 8192
PIECE = 32
PER = ROWS // PIECE
SCHEDULE = (
    ('y',),
    ('z', 0),
    ('t',),
    ('h',),
    ('z', 1),
    ('z', 2),
    ('x', 0),
    ('z', 3),
    ('z', 4),
    ('x', 1),
    ('z', 5),
    ('z', 6),
    ('x', 2),
    ('z', 7),
    ('z', 8),
    ('x', 3),
    ('x', 4),
    ('s', 0, 16),
    ('x', 5),
    ('x', 6),
    ('o', 0, 1),
    ('x', 7),
    ('o', 1, 3),
    ('x', 8),
    ('o', 3, 6),
    ('f',),
    ('n',),
    ('o', 6, 8),
    ('b', 0),
    ('o', 8, 9),
    ('b', 1),
    ('o', 9, 10),
    ('p', 0),
    ('a', 0),
    ('o', 10, 11),
    ('b', 2),
    ('o', 11, 12),
    ('p', 1),
    ('b', 3),
    ('o', 12, 13),
    ('a', 1),
    ('o', 13, 14),
    ('p', 2),
    ('o', 14, 16),
    ('a', 2),
    ('p', 3),
    ('a', 3),
)
SCALE = 1.0 / float(np.sqrt(np.float32(HD)))


def tables():
    position = np.arange(SEQ, dtype=np.float32)
    half = HD // 2
    freqs = np.power(np.float32(500000.0), -(np.arange(half, dtype=np.float32) * np.float32(2.0)) / np.float32(HD))
    angles = (position[:, None] * freqs[None, :].astype(np.float32)).astype(np.float32).astype(np.float64)
    cosine = np.cos(angles).astype(np.float32)
    sine = np.sin(angles).astype(np.float32)
    return np.concatenate([cosine, cosine], axis=1), np.concatenate([-sine, sine], axis=1)


def remote(src, dst, send, recv, device):
    return pltpu.make_async_remote_copy(
        src_ref=src, dst_ref=dst, send_sem=send, recv_sem=recv, device_id=device, device_id_type=MESH
    )


def kernel(
    hid_in, gain, qw, kw, vw, cos_in, sin_in, out,
    cos, sin, Z, W, H, HX, S1, ST, IV, NB, PO, SB, RB, KB, VB,
    ld, zr, zs, xr, xs, xfs, hx, w1s, s1r, s1s, s2r, s2s, opr, ops, hr, hs_, gr, gs, er, es, far,
):
    b = lax.axis_index("batch")
    t = lax.axis_index("tensor")
    x, l = b // 8, b % 8
    y, h, c = t // 4, (t // 2) % 2, t % 2
    z = 8 * h + l
    oc = 1 - c

    def dev(xx, yy, zz, cc):
        return (8 * xx + zz % 8, 4 * yy + 2 * (zz // 8) + cc)

    xp, xm = (x + 1) % 4, (x + 3) % 4
    yp, ym, yo = (y + 1) % 4, (y + 3) % 4, (y + 2) % 4
    zp, zm, zo = (z + 1) % 16, (z + 15) % 16, (z + 8) % 16
    z4p, z4m = (z + 4) % 16, (z + 12) % 16
    Dxp, Dxm = dev(xp, y, z, c), dev(xm, y, z, c)
    Dy = (dev(x, yp, z, c), dev(x, ym, z, c), dev(x, yo, z, c))
    Dzp, Dzm, Dzo = dev(x, y, zp, c), dev(x, y, zm, c), dev(x, y, zo, c)
    D4p, D4m = dev(x, y, z4p, c), dev(x, y, z4m, c)
    Dpart = dev(x, y, z, oc)
    ring = [(yt, cc) for yt in (yp, ym, yo) for cc in (c, oc)] + [(y, oc)]

    loads = [
        pltpu.make_async_copy(src, dst, ld.at[i])
        for i, (src, dst) in enumerate(
            [(hid_in.at[pl.ds(ROWS * r, ROWS)], H.at[y, h, r]) for r in range(CHUNKS)] + [(cos_in, cos), (sin_in, sin)]
        )
    ]
    for load in loads:
        load.start()

    barrier = pltpu.get_barrier_semaphore()
    peers = [Dzp, Dzm] + [dev(x, yt, z, cc) for yt, cc in ring]
    for cc in (c, oc):
        peers += [dev(xp, y, z, cc), dev(xm, y, z, cc), dev(x, y, z4p, cc), dev(x, y, z4m, cc)]
    for peer in peers:
        pl.semaphore_signal(barrier, inc=1, device_id=peer, device_id_type=MESH)

    S1[2 * y + c, 1] = gain[...].astype(F32).reshape(1, BLK)
    for r in range(CHUNKS):
        loads[r].wait()
        fold = None
        for g in range(4):
            v = H[y, h, r, :, pl.ds(128 * g, 128)].astype(F32)
            fold = v * v if fold is None else fold + v * v
        S1[2 * y + c, 0, :, pl.ds(ROWS * r, ROWS)] = jnp.sum(fold.T, axis=0, keepdims=True)

    pl.semaphore_wait(barrier, len(peers))
    pl.semaphore_signal(far, inc=1, device_id=D4m, device_id_type=MESH)

    row0 = pl.multiple_of(16 * c, 16)

    def pieces(yt):
        a0 = pl.multiple_of(1024 * yt, 512)
        b0 = pl.multiple_of(128 * yt, 128)
        rows = pl.ds(row0, 16)
        return (
            (qw.at[:, pl.ds(a0, 512)], Z.at[l, y, h, rows, pl.ds(0, 512)]),
            (kw.at[:, pl.ds(b0, 128)], Z.at[l, y, h, rows, pl.ds(512, 128)]),
            (vw.at[:, pl.ds(b0, 128)], Z.at[l, y, h, rows, pl.ds(640, 128)]),
            (qw.at[:, pl.ds(pl.multiple_of(a0 + 512, 512), 512)], Z.at[l, y, h, rows, pl.ds(768, 512)]),
        )

    for i, yt in enumerate((yp, ym, yo)):
        for src, dst in pieces(yt):
            remote(src, dst, w1s.at[i], zr.at[l, h, y], dev(x, yt, z, 0)).start()

    @pl.when(c == 0)
    def _():
        for src, dst in pieces(y):
            pltpu.make_async_copy(src, dst, zr.at[l, h, y]).start()

    @pl.when(c == 1)
    def _():
        for src, dst in pieces(y):
            remote(src, dst, w1s.at[3], zr.at[l, h, y], Dpart).start()

    for i, (yt, cc) in enumerate(ring):
        remote(S1.at[2 * y + c], S1.at[2 * y + c], s1s.at[i], s1r.at[2 * y + c], dev(x, yt, z, cc)).start()

    col0 = pl.multiple_of(512 * h, 512)

    def slot(s):
        ls, hs = s % 8, s // 8
        return (ls // 2) % 2, 2 * (ls // 4) + ls % 2, hs

    def need(s, k, d):
        sl, hs = s % 8, s // 8
        if d == 0:
            return sl + k < 8, 1 - hs
        return jnp.logical_and(k <= sl, sl != 7), jnp.where(sl == 7, hs, 1 - hs)

    def zeach(s, k, d, sub, act):
        ls, hs = s % 8, s // 8
        both, half = need(s, k, d)
        sems = (zs.at[d, ls, hs, sub], zr.at[ls, hs, sub], Dzp if d == 0 else Dzm)

        @pl.when(both)
        def _():
            ref = Z.at[ls, sub, hs]
            act(remote(ref, ref, *sems))

        @pl.when(jnp.logical_not(both))
        def _():
            ref = Z.at[ls, sub, hs, :, pl.ds(pl.multiple_of(512 * half, 512), 768)]
            act(remote(ref, ref, *sems))

    def start(copy):
        copy.start()

    def wait_recv(copy):
        copy.wait_recv()

    def wait_send(copy):
        copy.wait_send()

    def xcopy(s, sub, d):
        cc, lc, hs = slot(s)
        ls = s % 8
        return remote(
            Z.at[ls, sub, hs, :, pl.ds(col0, 768)], W.at[x, lc, sub, hs], xs.at[d, ls, hs, sub], xr.at[d, lc, hs, sub],
            dev((xp, xm, x)[d], y, z, cc),
        )

    def xfcopy(lc, hs, sub, d):
        ref = W.at[xm if d == 0 else xp, lc, sub, hs]
        return remote(ref, ref, xfs.at[lc, hs, sub], xr.at[3, lc, hs, sub], Dxp if d == 0 else Dxm)

    def zstep(k, d, sub):
        s = (z + 16 - k) % 16 if d == 0 else (z + k) % 16
        cc, lc, hs = slot(s)
        if k == 0:
            ref = Z.at[s % 8, sub, hs]
            remote(ref, ref, zs.at[0, s % 8, hs, sub], zr.at[s % 8, hs, sub], Dzp).wait_recv()
            zeach(s, 1, 0, sub, start)
            zeach(s, 1, 1, sub, start)
        else:
            zeach(s, k, d, sub, wait_recv)
            if k < 8 - d:
                zeach(s, k + 1, d, sub, start)
        xcopy(s, sub, 0).start()
        xcopy(s, sub, 1).start()

        @pl.when(cc == 1)
        def _():
            xcopy(s, sub, 2).start()

        @pl.when(cc == 0)
        def _():
            pltpu.make_async_copy(
                Z.at[s % 8, sub, hs, :, pl.ds(col0, 768)], W.at[x, lc, sub, hs], xr.at[2, lc, hs, sub]
            ).start()

    def xstep(k, d, sub, way):
        s = (z + 16 - k) % 16 if d == 0 else (z + k) % 16
        cc, lc, hs = slot(s)

        @pl.when(cc == c)
        def _():
            xcopy(s, sub, way).wait_recv()
            xfcopy(lc, hs, sub, way).start()

    def zround(k):
        @pl.when(c == 0)
        def _():
            def body(sub, carry):
                zstep(k, 0, sub)
                if 0 < k < 8:
                    zstep(k, 1, sub)
                return carry

            lax.fori_loop(0, 4, body, 0)

    def xround(k, first=0, last=2):
        def body(i, carry):
            for j in range(2):
                xstep(k, 0, 2 * i + j, j)
                if 0 < k < 8:
                    xstep(k, 1, 2 * i + j, j)
            return carry

        lax.fori_loop(first, last, body, 0)

    def hcopy(r, d):
        ref = H.at[y, h, r]
        return remote(ref, ref, hs_.at[d, r], hr.at[d, r], Dy[d])

    def hwait(r, d):
        hcopy(r, d).wait_recv()

    def ocopy(p, cc):
        part = (p // PER, pl.ds(PIECE * (p % PER), PIECE))
        src = H.at[y, h, part[0], part[1]] if cc == 1 else HX.at[part[0], part[1]]
        return remote(src, H.at[y, h, part[0], part[1]], ops.at[cc, p], opr.at[p], dev(x, y, zo, cc))

    pushed = remote(H.at[y, h], HX, hx.at[0], hx.at[1], Dpart)

    def push():
        @pl.when(c == 0)
        def _():
            pushed.start()

        @pl.when(c == 1)
        def _():
            pushed.wait_recv()

    def across(first, last):
        @pl.when(c == 1)
        def _():
            def body(p, carry):
                ocopy(p, 1).start()
                ocopy(p, 0).start()
                return carry

            lax.fori_loop(first, last, body, 0)

    def gcopy(p, d):
        ref = H.at[y, 1 - h, p // PER, pl.ds(PIECE * (p % PER), PIECE)]
        return remote(ref, ref, gs.at[d, p], gr.at[d, p], Dy[d])

    def opposite(p):
        ocopy(p, 1).wait_recv()
        for d in (2, 0, 1):
            gcopy(p, d).start()

    s2copy = remote(ST.at[0], ST.at[1], s2s.at[0], s2r.at[0], Dzo)

    def stats():
        for yt, cc in ring:
            remote(S1.at[2 * yt + cc], S1.at[2 * yt + cc], s1s.at[0], s1r.at[2 * yt + cc], Dpart).wait_recv()
        part = S1[0, 0]
        for i in range(1, 8):
            part = part + S1[i, 0]
        ST[0, 0] = part
        for i in range(4):
            ST[0, 1 + i] = S1[2 * i + c, 1]
        pl.semaphore_wait(far, 1)
        s2copy.start()

    def scales():
        s2copy.wait_recv()
        total = ST[0, 0] + ST[1, 0]
        for r in range(CHUNKS):
            wide = jnp.broadcast_to(total[:, ROWS * r : ROWS * (r + 1)], (ROWS, ROWS)).T
            IV[r] = lax.rsqrt(wide / D + 1e-05)

    def normalize(r, hb, side):
        for rel in range(4):
            yb = (x + rel) % 4
            for g in range(4):
                v = H[yb, hb, r, :, pl.ds(128 * g, 128)].astype(F32)
                scale = ST[side, 1 + yb, :, pl.ds(128 * g, 128)]
                NB[:, pl.ds(512 * rel + 128 * g, 128)] = (v * IV[r] * scale).astype(BF16)

    off_own = 256 * h + 256 * c
    off_oth = 256 * h + 256 * oc
    off_kv = 512 * (1 - h)

    def group(hb, off):
        acc = None
        for rel in range(4):
            yb = (x + rel) % 4
            lhs = NB[:, pl.ds(512 * rel, 512)]
            rhs = W[yb, pl.ds(2 * hb, 2), :, :, :, pl.ds(pl.multiple_of(off, 256), 256)]
            prod = jnp.dot(lhs, rhs.reshape(512, 256), preferred_element_type=F32)
            acc = prod if acc is None else acc + prod
        return acc

    def ecopy(r):
        return remote(SB.at[r], RB.at[r], es.at[r], er.at[r], Dpart)

    def begin(r):
        for d in range(3):
            hwait(r, d)
        normalize(r, h, 0)
        SB[r, :, pl.ds(0, 256)] = group(h, off_oth)
        SB[r, :, pl.ds(256, 256)] = group(h, off_kv)
        PO[r, :, pl.ds(0, 256)] = group(h, off_own)

    def project(r):
        for d in range(3):
            for p in range(PER * r, PER * (r + 1)):
                gcopy(p, d).wait_recv()
        normalize(r, 1 - h, 1)
        SB[r, :, pl.ds(0, 256)] += group(1 - h, off_oth)
        kv = SB[r, :, pl.ds(256, 256)] + group(1 - h, off_kv)
        SB[r, :, pl.ds(256, 256)] = kv
        ecopy(r).start()
        PO[r, :, pl.ds(256, 256)] = kv
        PO[r, :, pl.ds(0, 256)] += group(1 - h, off_own)

    def rotated(v, r):
        co = cos[pl.ds(ROWS * r, ROWS), :]
        si = sin[pl.ds(ROWS * r, ROWS), :]
        return (v * co + pltpu.roll(v, 64, 1) * si).astype(BF16)

    def attend(r):
        ecopy(r).wait_recv()

        def summed(j):
            return PO[r, :, pl.ds(128 * j, 128)] + RB[r, :, pl.ds(128 * j, 128)]

        KB[pl.ds(ROWS * r, ROWS), :] = rotated(summed(2), r)
        VB[pl.ds(ROWS * r, ROWS), :] = summed(3).astype(BF16)
        n = ROWS * (r + 1)
        keys = KB[pl.ds(0, n), :]
        vals = VB[pl.ds(0, n), :]
        row = lax.broadcasted_iota(jnp.int32, (ROWS, n), 0) + ROWS * r
        col = lax.broadcasted_iota(jnp.int32, (ROWS, n), 1)
        for j in range(2):
            query = rotated(summed(j), r)
            sc = lax.dot_general(query, keys, (((1,), (1,)), ((), ())), preferred_element_type=F32) * SCALE
            sc = jnp.where(col <= row, sc, F32(-1e30))
            top = jnp.max(sc, axis=1, keepdims=True)
            ex = jnp.exp(sc - top)
            probs = (ex / jnp.sum(ex, axis=1, keepdims=True)).astype(BF16)
            out[pl.ds(ROWS * r, ROWS), pl.ds(HD * j, HD)] = jnp.dot(probs, vals, preferred_element_type=F32).astype(BF16)

    def wfinish():
        def body(i, carry):
            lc, hs = i // 2, i % 2
            for sub in range(4):
                source = 8 * hs + 4 * (lc // 2) + 2 * c + lc % 2
                xcopy(source, sub, 1 - sub % 2).wait_recv()
                xcopy(source, sub, 2).wait_recv()
                xfcopy(lc, hs, sub, 0).wait_recv()
            return carry

        lax.fori_loop(0, 8, body, 0)

    def rope_tables():
        loads[CHUNKS].wait()
        loads[CHUNKS + 1].wait()

    for step in SCHEDULE:
        name, args = step[0], step[1:]
        if name == "z":
            zround(*args)
        elif name == "x":
            xround(*args)
        elif name == "t":
            stats()
        elif name == "n":
            scales()
        elif name == "y":
            for r in range(CHUNKS):
                for d in range(3):
                    hcopy(r, d).start()
        elif name == "h":
            push()
        elif name == "s":
            across(*args)
        elif name == "o":
            for p in range(*args):
                opposite(p)
        elif name == "f":
            wfinish()
            rope_tables()
        elif name == "b":
            begin(*args)
        elif name == "p":
            project(*args)
        else:
            attend(*args)

    piece16 = Z.at[0, 0, 0, pl.ds(0, 16)]
    for i in range(3):
        remote(piece16, piece16, w1s.at[i], s1r.at[0], Dpart).wait_send()

    @pl.when(c == 1)
    def _():
        remote(piece16, piece16, w1s.at[3], s1r.at[0], Dpart).wait_send()

    for i in range(7):
        remote(S1.at[0], S1.at[0], s1s.at[i], s1r.at[0], Dpart).wait_send()
    s2copy.wait_send()

    def zdone(d):
        def body(k, carry):
            s = (z + 16 - k) % 16 if d == 0 else (z + k) % 16
            for sub in range(4):
                zeach(s, k + 1, d, sub, wait_send)
            return carry

        lax.fori_loop(0, 8 - d, body, 0)

    @pl.when(c == 0)
    def _():
        pushed.wait_send()
        zdone(0)
        zdone(1)

        def xdone(s, carry):
            for sub in range(4):
                xcopy(s, sub, 0).wait_send()
                xcopy(s, sub, 1).wait_send()

                @pl.when(slot(s)[0] == 1)
                def _():
                    xcopy(s, sub, 2).wait_send()

            return carry

        lax.fori_loop(0, 16, xdone, 0)

    def xfdone(i, carry):
        for sub in range(4):
            xfcopy(i // 2, i % 2, sub, 0).wait_send()
        return carry

    lax.fori_loop(0, 8, xfdone, 0)
    for r in range(CHUNKS):
        ecopy(r).wait_send()
        for d in range(3):
            hcopy(r, d).wait_send()

    def pdone(p, carry):
        @pl.when(c == 1)
        def _():
            ocopy(p, 0).wait_send()
            ocopy(p, 1).wait_send()

        for d in range(3):
            gcopy(p, d).wait_send()
        return carry

    lax.fori_loop(0, PER * CHUNKS, pdone, 0)


def on_device(hidden_in, norm_gain, q_weight, k_weight, v_weight):
    cos, sin = tables()
    dma = pltpu.SemaphoreType.DMA
    vmem = pltpu.VMEM
    hbm = pl.BlockSpec(memory_space=pltpu.HBM)
    return pl.pallas_call(
        kernel,
        out_shape=jax.ShapeDtypeStruct((SEQ, 256), BF16),
        in_specs=[hbm, pl.BlockSpec(memory_space=vmem), hbm, hbm, hbm, hbm, hbm],
        out_specs=pl.BlockSpec(memory_space=vmem),
        scratch_shapes=[
            vmem((SEQ, HD), F32),
            vmem((SEQ, HD), F32),
            vmem((8, 4, 2, 32, 1280), BF16),
            vmem((4, 4, 4, 2, 32, 768), BF16),
            vmem((4, 2, CHUNKS, ROWS, BLK), BF16),
            vmem((CHUNKS, ROWS, BLK), BF16),
            vmem((8, 2, 1, SEQ), F32),
            vmem((2, 5, 1, SEQ), F32),
            vmem((CHUNKS, ROWS, ROWS), F32),
            vmem((ROWS, 4 * BLK), BF16),
            vmem((CHUNKS, ROWS, 512), F32),
            vmem((CHUNKS, ROWS, 512), F32),
            vmem((CHUNKS, ROWS, 512), F32),
            vmem((SEQ, HD), BF16),
            vmem((SEQ, HD), BF16),
            dma((CHUNKS + 2,)),
            dma((8, 2, 4)),
            dma((2, 8, 2, 4)),
            dma((4, 4, 2, 4)),
            dma((3, 8, 2, 4)),
            dma((4, 2, 4)),
            dma((2,)),
            dma((4,)),
            dma((8,)),
            dma((7,)),
            dma((1,)),
            dma((1,)),
            dma((PER * CHUNKS,)),
            dma((2, PER * CHUNKS)),
            dma((3, CHUNKS)),
            dma((3, CHUNKS)),
            dma((3, PER * CHUNKS)),
            dma((3, PER * CHUNKS)),
            dma((CHUNKS,)),
            dma((CHUNKS,)),
            pltpu.SemaphoreType.REGULAR,
        ],
        compiler_params=pltpu.CompilerParams(
            collective_id=0, has_side_effects=True, vmem_limit_bytes=67043328
        ),
    )(hidden_in, norm_gain, q_weight, k_weight, v_weight, jnp.asarray(cos), jnp.asarray(sin))


def solution(mesh):
    placed = (
        P("batch", "tensor"),
        P("tensor"),
        P(("batch", "tensor"), None),
        P(("batch", "tensor"), None),
        P(("batch", "tensor"), None),
    )
    return jax.shard_map(
        on_device, mesh=mesh, in_specs=placed, out_specs=P("batch", "tensor"), check_vma=False
    )
```
